1024 devices in a mesh: expert: 64 (over z, y), dp: 16 (over x, core).
Axes of the slice: x: 8, y: 8, z: 8, core: 2. Of those that a mesh axis runs over, the one named last changes fastest.
Arguments:
- cotangent: bfloat16 [131072, 2048], P(('expert', 'dp')), may hold values from -4 to 4
- router_probs: bfloat16 [131072, 1], P(('expert', 'dp')), may hold values from 0.049804688 to 0.59765625
- slot_ids: int32 [131072, 1], P(('expert', 'dp')), may hold values from 0 to 63; in each aligned block of 128 rows (0 to 127, 128 to 255, ...) at most 3 rows name the same one
- saved_hidden: bfloat16 [64, 3072, 1024], P('expert', 'dp'), may hold values from -6 to 6
- down_weight: bfloat16 [64, 2048, 512], P('expert', 'dp'), as said below
Outputs:
- grad_down: float32 [64, 2048, 512], P('expert', 'dp')
- grad_hidden: bfloat16 [64, 3072, 1024], P('expert', 'dp')
- grad_probs: float32 [131072, 1], P(('expert', 'dp'))
The draws below stay inside these ranges and needn't reach their ends.
Inputs may be any that keep to these rules, and one draw needn't show every extreme that they name: `slot_ids`: in the 128 tokens of one device, each token names one slot, no slot is named by more than 3 tokens, a bound that some block reaches. `down_weight`: slots s and s + 32 hold the same expert's weights.
All inputs are finite; a program needn't handle non-finite values.
Results may differ from the reference program's by a relative error of at most 0.007.
Values may be sent and summed in bfloat16 or wider, within the bound.
No kernel may reach another device: no remote copies, remote signals or barrier semaphores. Data moves between devices by JAX's collectives and lax.ppermute only.
A program may use at most 32 MiB of HBM per device.

```python
import math
import jax
import jax.numpy as jnp
import numpy as np
from jax import lax

D = 2048
FF = 512
TOP = 1
TOK_DEV = 128
EXPERTS = 32
SLOTS = 64
CAP = 3
ROWS = 3072
TOKENS = 131072
N_EXPERT = 64
N_DP = 16
DEVICES = 1024


def draw_down_weight(key, part):
    base_weight = jax.random.normal(jax.random.fold_in(key, 17), (EXPERTS, D, FF), jnp.float32) * FF ** (-0.5)
    return jnp.concatenate([base_weight, base_weight], axis=0).astype(jnp.bfloat16)


def steps_of(stream_key, dims, split, smallest, high):
    gain, own = 1.0, jax.random.fold_in(stream_key, 6)
    for dim, shards_of in split:
        steps = jnp.exp(jax.random.uniform(jax.random.fold_in(own, dim), (shards_of,), jnp.float32, smallest / len(split), high / len(split)))
        gain = gain * jnp.repeat(steps, dims[dim] // shards_of).reshape([-1 if axis == dim else 1 for axis in range(len(dims))])
    return gain


def routed_block(own_key, own, number, rows, count, top, reach, lean):
    ranking = jax.random.permutation(own_key, count)
    heavy_load, ordinary = shares(count, rows * top, reach, lean, True), shares(count, rows * top, reach, lean, False)
    places = jnp.arange(count)

    def named(tallies, offset_by):
        used = int((tallies > 0).sum())
        fixed = max(1, used // 4)
        moved = fixed + (places - fixed + offset_by * (used - fixed)) % max(1, count - fixed)
        return jnp.zeros((count,), jnp.int32).at[ranking[jnp.where(places < fixed, places, moved)]].set(jnp.asarray(tallies, jnp.int32))

    tallies = jnp.where(number % 4 == 0, named(heavy_load, number // 4), named(ordinary, number - number // 4 - 1))
    mixed = jax.random.permutation(jax.random.fold_in(own, 3), count)
    giver, receiver = mixed[0:count // 2 * 2:2], mixed[1:count // 2 * 2:2]
    margin = jnp.minimum(tallies[giver] - 1, reach - tallies[receiver]) // 2
    margin = jnp.where((giver == ranking[0]) | (receiver == ranking[0]) | (tallies[receiver] == 0), 0, jnp.maximum(margin, 0))
    moved = jax.random.randint(jax.random.fold_in(own, 4), (count // 2,), 0, 1 << 20) % (margin + 1)
    tallies = tallies.at[giver].add(-moved).at[receiver].add(moved)
    labels = jnp.searchsorted(jnp.cumsum(tallies), jnp.arange(rows * top), side="right").astype(jnp.int32)
    grid = labels.reshape(top, rows).T
    grid = grid[jax.random.permutation(jax.random.fold_in(own, 1), rows)]
    offset_by = jax.random.randint(jax.random.fold_in(own, 2), (rows, 1), 0, top)
    return jnp.take_along_axis(grid, (jnp.arange(top)[None, :] + offset_by) % top, axis=1)


def shares(count, total, limit, slope, full):
    weights = [(1 << 20) // math.isqrt(rank ** slope) + 1 for rank in range(1, count + 1)]
    largest = limit if full else min(limit, max(-(-total // count), total * weights[0] // sum(weights)))
    least = 1 if total - largest >= count - 1 else 0
    given, surplus = [largest] + [least] * (count - 1), total - largest - least * (count - 1)
    while surplus > 0:
        free = [i for i in range(1, count) if given[i] < largest] or [i for i in range(1, count) if given[i] < limit]
        mass, remaining = sum([weights[i] for i in free]), surplus
        for i in free:
            extra = min(limit - given[i], max(1, remaining * weights[i] // mass), surplus)
            given[i] = given[i] + extra
            surplus = surplus - extra
    return np.array(given)


def normal_values(rng, extent, spread, most, cuts=(), kind=jnp.bfloat16):
    array = spread * jax.random.normal(rng, extent, jnp.float32)
    if cuts:
        array = array * steps_of(rng, extent, cuts, -0.22, 0.18)
    return jnp.clip(array, -most, most).astype(kind)


def setup_inputs(seed: int = 0) -> dict:
    key_of = jax.random.split(jax.random.key(seed), 6)
    cotangent = normal_values(key_of[0], (TOKENS, D), 0.25, 4.0, ((0, 1024),))
    router_probs = jnp.clip(0.049804688 + 0.54785156 * jax.random.uniform(key_of[1], (TOKENS, TOP), jnp.float32) ** steps_of(key_of[1], (TOKENS, TOP), ((0, 1024),), -0.2, 0.2), 0.049804688, 0.59765625).astype(jnp.bfloat16)
    slot_ids_keys = jax.random.split(jax.random.fold_in(key_of[2], 1), TOKENS // TOK_DEV)
    slot_ids_turns = jax.random.permutation(jax.random.fold_in(key_of[2], 3), TOKENS // TOK_DEV)
    slot_ids = jax.vmap(lambda own, number: routed_block(jax.random.fold_in(key_of[2], 2), own, number, TOK_DEV, SLOTS, TOP, CAP, 2))(slot_ids_keys, slot_ids_turns).reshape((TOKENS, TOP))
    saved_hidden = normal_values(key_of[3], (SLOTS, ROWS, 2 * FF), 1.0, 6.0, ((0, 64), (1, 16)))
    down_weight = draw_down_weight(jax.random.fold_in(key_of[5], 71), 0)
    return {"cotangent": cotangent, "router_probs": router_probs, "slot_ids": slot_ids, "saved_hidden": saved_hidden, "down_weight": down_weight}


def reference(cotangent, router_probs, slot_ids, saved_hidden, down_weight):
    pair_count = TOK_DEV * TOP
    dev_slots = slot_ids.reshape(DEVICES, pair_count)
    slot_range = jnp.arange(SLOTS, dtype=jnp.int32)
    slot_hits = (dev_slots[:, :, None] == slot_range[None, None, :]).astype(jnp.int32)
    earlier = jnp.cumsum(slot_hits, axis=1) - slot_hits
    position = jnp.sum(earlier * slot_hits, axis=2).astype(jnp.int32)
    device_ids = jnp.arange(DEVICES, dtype=jnp.int32)
    exp_index = device_ids // N_DP
    dp_index = device_ids % N_DP
    row_index = (dp_index[:, None] * (N_EXPERT * CAP) + exp_index[:, None] * CAP + position).astype(jnp.int32)
    flat_slot = dev_slots.reshape(-1).astype(jnp.int32)
    flat_row = row_index.reshape(-1).astype(jnp.int32)
    flat_place = (flat_slot * ROWS + flat_row).astype(jnp.int32)
    table = jnp.full((SLOTS * ROWS,), -1, dtype=jnp.int32)
    table = table.at[flat_place].set(jnp.arange(TOKENS * TOP, dtype=jnp.int32))
    table = table.reshape(SLOTS, ROWS)
    flat_probs = router_probs.reshape(-1)

    def per_slot(inputs):
        pair_ids, hidden, weight = inputs
        valid = pair_ids >= 0
        safe_ids = jnp.maximum(pair_ids, 0).astype(jnp.int32)
        cot_rows = jnp.where(valid[:, None], cotangent[safe_ids // TOP], jnp.zeros((), cotangent.dtype))
        prob_rows = jnp.where(valid, flat_probs[safe_ids], jnp.zeros((), flat_probs.dtype))
        gate_pre = hidden[:, :FF].astype(jnp.float32)
        up_pre = hidden[:, FF:].astype(jnp.float32)
        gate_sig = jax.nn.sigmoid(gate_pre)
        gate_act = gate_pre * gate_sig
        activation = (gate_act * up_pre).astype(jnp.bfloat16)
        outputs = lax.dot_general(activation, weight, (((1,), (1,)), ((), ())), preferred_element_type=jnp.float32)
        prob_grad = jnp.sum(cot_rows.astype(jnp.float32) * outputs, axis=1)
        scaled = (prob_rows.astype(jnp.float32)[:, None] * cot_rows.astype(jnp.float32)).astype(jnp.bfloat16)
        grad_act = jnp.dot(scaled, weight, preferred_element_type=jnp.float32)
        grad_gate = grad_act * up_pre * gate_sig * (1.0 + gate_pre * (1.0 - gate_sig))
        grad_up = grad_act * gate_act
        grad_hidden = jnp.concatenate([grad_gate, grad_up], axis=1).astype(jnp.bfloat16)
        weight_grad = lax.dot_general(scaled, activation, (((0,), (0,)), ((), ())), preferred_element_type=jnp.float32)
        return weight_grad, grad_hidden, prob_grad

    weight_grads, grad_hidden, prob_grads = lax.map(per_slot, (table, saved_hidden, down_weight))
    grad_down = weight_grads + jnp.roll(weight_grads, EXPERTS, axis=0)
    grad_probs = prob_grads.reshape(-1)[flat_place].reshape(TOKENS, TOP)
    return grad_down, grad_hidden, grad_probs
```

```python
import jax
import jax.numpy as jnp
from jax import lax
from jax.sharding import Mesh, PartitionSpec as P


BF = jnp.bfloat16
F32 = jnp.float32
SPREAD = ("core", "expert")


def swap(block, axis, bit):
    count = lax.axis_size(axis)
    return lax.ppermute(block, axis, [(k, k ^ bit) for k in range(count)])


def shift(block, axis, step):
    count = lax.axis_size(axis)
    return lax.ppermute(block, axis, [(k, (k + step) % count) for k in range(count)])


def exchange(blocks, axis):
    return lax.all_to_all(blocks, axis, split_axis=0, concat_axis=0, tiled=True)


def swiglu(hidden):
    ff = hidden.shape[1] // 2
    gate = hidden[:, :ff].astype(F32)
    up = hidden[:, ff:].astype(F32)
    sig = jax.nn.sigmoid(gate)
    silu = gate * sig
    return gate, up, sig, silu, (silu * up).astype(BF)


def on_device(cotangent, router_probs, slot_ids, saved_hidden, down_weight):
    slots = lax.axis_size("expert")
    chips = lax.axis_size("x")
    core = lax.axis_index("core")
    tokens, width = cotangent.shape
    cap = saved_hidden.shape[1] // slots
    lanes = width // (2 * chips)
    rows = slots * cap
    first = core == 0
    hidden = saved_hidden[0]
    ff = hidden.shape[1] // 2

    ids = slot_ids.reshape(-1)
    same = (ids[:, None] == ids[None, :]) & (
        jnp.arange(tokens)[None, :] < jnp.arange(tokens)[:, None]
    )
    position = jnp.sum(same.astype(jnp.int32), axis=1)
    target = ids * cap + position
    place = target[:, None] == jnp.arange(rows, dtype=jnp.int32)[None, :]
    probs = router_probs.astype(F32)
    spread = jnp.where(place, probs, 0.0).astype(BF)
    sent = lax.dot_general(
        spread, cotangent, (((0,), (0,)), ((), ())), preferred_element_type=F32
    ).astype(BF)
    sent = sent.reshape(slots, cap, chips, 2, lanes).transpose(3, 0, 1, 2, 4)
    sent = sent.reshape(2 * slots, cap * chips, lanes)
    got = exchange(sent, SPREAD)
    scaled = got.reshape(2 * rows, chips * lanes)

    chip = lax.axis_index("x")
    weight = jnp.zeros((chips,) + down_weight.shape[1:], BF)
    weight = lax.dynamic_update_index_in_dim(weight, down_weight[0], chip, 0)
    for step in range(1, chips):
        block = shift(down_weight[0], "x", step)
        weight = lax.dynamic_update_index_in_dim(
            weight, block, jnp.bitwise_and(chip - step, chips - 1), 0
        )
    weight = weight.reshape(chips * lanes, ff)

    activation = swiglu(hidden)[-1]
    other_activation = swap(activation, "core", 1)
    both = jnp.concatenate(
        [
            jnp.where(first, activation, other_activation),
            jnp.where(first, other_activation, activation),
        ],
        axis=0,
    )

    partial = lax.dot_general(
        scaled, both, (((0,), (0,)), ((), ())), preferred_element_type=F32
    ).astype(BF)
    parts = exchange(partial.reshape(chips, lanes, ff), "x")
    slot_grad = jnp.sum(parts.astype(F32), axis=0)
    rounded = slot_grad.astype(BF)
    partner = swap(rounded, "expert", slots // 2)
    grad_down = (slot_grad + partner.astype(F32))[None]

    half = jnp.dot(scaled, weight, preferred_element_type=F32)
    low, high = half[:rows], half[rows:]
    mine = jnp.where(first, low, high)
    theirs = jnp.where(first, high, low)
    theirs = swap(theirs, "core", 1)
    hidden, theirs = lax.optimization_barrier((hidden, theirs))
    gate, up, sig, silu, activation = swiglu(hidden)
    grad_act = mine + theirs
    grad_gate = grad_act * up * sig * (1.0 + gate * (1.0 - sig))
    grad_up = grad_act * silu
    grad_hidden = jnp.concatenate([grad_gate, grad_up], axis=1).astype(BF)[None]
    weighted = jnp.sum(grad_act * activation.astype(F32), axis=1)
    back = exchange(weighted.reshape(slots, cap), "expert").reshape(rows)
    grad_probs = (
        jnp.sum(jnp.where(place, back[None, :], 0.0), axis=1, keepdims=True) / probs
    )
    return (grad_down, grad_hidden, grad_probs)


def solution(mesh):
    slots, groups = mesh.shape["expert"], mesh.shape["dp"]
    fine = Mesh(mesh.devices.reshape(slots, groups // 2, 2), ("expert", "x", "core"))
    dp = ("x", "core")
    tok = P(("expert", "x", "core"), None)
    slot = P("expert", dp, None)

    return jax.shard_map(
        on_device,
        mesh=fine,
        in_specs=(tok, tok, tok, slot, slot),
        out_specs=(slot, slot, tok),
        check_vma=False,
    )
```

```python
import jax
import jax.numpy as jnp
from jax import lax
from jax.sharding import Mesh, PartitionSpec as P


BF = jnp.bfloat16
F32 = jnp.float32
SPREAD = ("core", "expert")


def swap(block, axis, bit):
    count = lax.axis_size(axis)
    return lax.ppermute(block, axis, [(k, k ^ bit) for k in range(count)])


def fan(block, step):
    chips = lax.axis_size("x")
    route = [
        (chip * 2 + core, (chip + step - 2 * step * core) % chips * 2 + core)
        for chip in range(chips)
        for core in range(2)
    ]
    return lax.ppermute(block, ("x", "core"), route)


def exchange(blocks, axis):
    return lax.all_to_all(blocks, axis, split_axis=0, concat_axis=0, tiled=True)


def swiglu(hidden):
    ff = hidden.shape[1] // 2
    gate = hidden[:, :ff].astype(F32)
    up = hidden[:, ff:].astype(F32)
    sig = jax.nn.sigmoid(gate)
    silu = gate * sig
    return gate, up, sig, silu, (silu * up).astype(BF)


def on_device(cotangent, router_probs, slot_ids, saved_hidden, down_weight):
    slots = lax.axis_size("expert")
    chips = lax.axis_size("x")
    core = lax.axis_index("core")
    tokens, width = cotangent.shape
    cap = saved_hidden.shape[1] // slots
    lanes = width // (2 * chips)
    rows = slots * cap
    first = core == 0
    hidden = saved_hidden[0]
    ff = hidden.shape[1] // 2

    ids = slot_ids.reshape(-1)
    same = (ids[:, None] == ids[None, :]) & (
        jnp.arange(tokens)[None, :] < jnp.arange(tokens)[:, None]
    )
    position = jnp.sum(same.astype(jnp.int32), axis=1)
    target = ids * cap + position
    place = target[:, None] == jnp.arange(rows, dtype=jnp.int32)[None, :]
    probs = router_probs.astype(F32)
    spread = jnp.where(place, probs, 0.0).astype(BF)
    sent = lax.dot_general(
        spread, cotangent, (((0,), (0,)), ((), ())), preferred_element_type=F32
    ).astype(BF)
    sent = sent.reshape(slots, cap, chips, 2, lanes).transpose(3, 0, 1, 2, 4)
    sent = sent.reshape(2 * slots, cap * chips, lanes)
    got = exchange(sent, SPREAD)
    scaled = got.reshape(2 * rows, chips * lanes)

    chip = lax.axis_index("x")
    ahead = jnp.where(first, -1, 1)
    mate = swap(down_weight[0], "core", 1)
    pair = jnp.concatenate([down_weight, mate[None]], axis=0)
    pieces = {0: down_weight[0]}
    relayed = []
    for step in range(1, chips // 2):
        got_pair = fan(pair, step)
        pieces[step] = got_pair[0]
        relayed.append(got_pair[1])
    far = fan(down_weight[0], chips // 2)
    pieces[chips // 2] = far
    relayed = swap(jnp.stack(relayed), "core", 1)
    for step in range(1, chips // 2):
        pieces[-step] = relayed[step - 1]
    weight = jnp.zeros((chips,) + down_weight.shape[1:], BF)
    for step, piece in pieces.items():
        weight = lax.dynamic_update_index_in_dim(
            weight, piece, jnp.bitwise_and(chip + ahead * step, chips - 1), 0
        )
    weight = weight.reshape(chips * lanes, ff)

    activation = swiglu(hidden)[-1]
    other_activation = swap(activation, "core", 1)
    both = jnp.concatenate(
        [
            jnp.where(first, activation, other_activation),
            jnp.where(first, other_activation, activation),
        ],
        axis=0,
    )

    partial = lax.dot_general(
        scaled, both, (((0,), (0,)), ((), ())), preferred_element_type=F32
    ).astype(BF)
    parts = exchange(partial.reshape(chips, lanes, ff), "x")
    slot_grad = jnp.sum(parts.astype(F32), axis=0)
    rounded = slot_grad.astype(BF)
    partner = swap(rounded, "expert", slots // 2)
    grad_down = (slot_grad + partner.astype(F32))[None]

    half = jnp.dot(scaled, weight, preferred_element_type=F32)
    low, high = half[:rows], half[rows:]
    mine = jnp.where(first, low, high)
    theirs = jnp.where(first, high, low)
    theirs = swap(theirs, "core", 1)
    hidden, theirs = lax.optimization_barrier((hidden, theirs))
    gate, up, sig, silu, activation = swiglu(hidden)
    grad_act = mine + theirs
    grad_gate = grad_act * up * sig * (1.0 + gate * (1.0 - sig))
    grad_up = grad_act * silu
    grad_hidden = jnp.concatenate([grad_gate, grad_up], axis=1).astype(BF)[None]
    weighted = jnp.sum(grad_act * activation.astype(F32), axis=1)
    back = exchange(weighted.reshape(slots, cap), "expert").reshape(rows)
    grad_probs = (
        jnp.sum(jnp.where(place, back[None, :], 0.0), axis=1, keepdims=True) / probs
    )
    return (grad_down, grad_hidden, grad_probs)


def solution(mesh):
    slots, groups = mesh.shape["expert"], mesh.shape["dp"]
    fine = Mesh(mesh.devices.reshape(slots, groups // 2, 2), ("expert", "x", "core"))
    dp = ("x", "core")
    tok = P(("expert", "x", "core"), None)
    slot = P("expert", dp, None)

    return jax.shard_map(
        on_device,
        mesh=fine,
        in_specs=(tok, tok, tok, slot, slot),
        out_specs=(slot, slot, tok),
        check_vma=False,
    )
```

```python
import jax
import jax.numpy as jnp
import numpy as np
from jax import lax
from jax.sharding import Mesh, PartitionSpec as P


BF = jnp.bfloat16
F32 = jnp.float32
SPREAD = ("core", "expert")


def swap(block, axis, bit):
    count = lax.axis_size(axis)
    return lax.ppermute(block, axis, [(k, k ^ bit) for k in range(count)])


def fan(block):
    chips = lax.axis_size("x")
    route = [
        (chip * 2 + core, (chip + 1 - 2 * core) % chips * 2 + core)
        for chip in range(chips)
        for core in range(2)
    ]
    return lax.ppermute(block, ("x", "core"), route)


def exchange(blocks, axis):
    return lax.all_to_all(blocks, axis, split_axis=0, concat_axis=0, tiled=True)


def swiglu(hidden):
    ff = hidden.shape[1] // 2
    gate = hidden[:, :ff].astype(F32)
    up = hidden[:, ff:].astype(F32)
    sig = jax.nn.sigmoid(gate)
    silu = gate * sig
    return gate, up, sig, silu, (silu * up).astype(BF)


def on_device(cotangent, router_probs, slot_ids, saved_hidden, down_weight):
    slots = lax.axis_size("expert")
    chips = lax.axis_size("x")
    core = lax.axis_index("core")
    tokens, width = cotangent.shape
    cap = saved_hidden.shape[1] // slots
    lanes = width // (2 * chips)
    rows = slots * cap
    first = core == 0
    hidden = saved_hidden[0]
    ff = hidden.shape[1] // 2

    ids = slot_ids.reshape(-1)
    same = (ids[:, None] == ids[None, :]) & (
        jnp.arange(tokens)[None, :] < jnp.arange(tokens)[:, None]
    )
    position = jnp.sum(same.astype(jnp.int32), axis=1)
    row = np.arange(rows, dtype=np.int32)
    place = (ids[:, None] == (row // cap)[None, :]) & (
        position[:, None] == (row % cap)[None, :]
    )
    probs = router_probs.astype(F32)
    spread = jnp.where(place, probs, 0.0).astype(BF)
    sent = lax.dot_general(
        spread, cotangent, (((0,), (0,)), ((), ())), preferred_element_type=F32
    ).astype(BF)
    sent = sent.reshape(slots, cap, chips, 2, lanes).transpose(3, 0, 1, 2, 4)
    sent = sent.reshape(2 * slots, cap * chips, lanes)
    got = exchange(sent, SPREAD)
    scaled = got.reshape(2 * rows, chips * lanes)

    chip = lax.axis_index("x")
    ahead = jnp.where(first, -1, 1)
    mate = swap(down_weight[0], "core", 1)
    pair = jnp.concatenate([down_weight, mate[None]], axis=0)
    pieces = {0: down_weight[0]}
    relayed = []
    moving = pair
    for step in range(1, chips // 2):
        moving = fan(moving)
        pieces[step] = moving[0]
        relayed.append(moving[1])
    far = fan(moving)
    pieces[chips // 2] = far[0]
    relayed = swap(jnp.stack(relayed), "core", 1)
    for step in range(1, chips // 2):
        pieces[-step] = relayed[step - 1]
    weight = jnp.zeros((chips,) + down_weight.shape[1:], BF)
    for step, piece in pieces.items():
        weight = lax.dynamic_update_index_in_dim(
            weight, piece, jnp.bitwise_and(chip + ahead * step, chips - 1), 0
        )
    weight = weight.reshape(chips * lanes, ff)

    activation = swiglu(hidden)[-1]
    other_activation = swap(activation, "core", 1)
    both = jnp.concatenate(
        [
            jnp.where(first, activation, other_activation),
            jnp.where(first, other_activation, activation),
        ],
        axis=0,
    )

    partial = lax.dot_general(
        scaled, both, (((0,), (0,)), ((), ())), preferred_element_type=F32
    ).astype(BF)
    parts = exchange(partial.reshape(chips, lanes, ff), "x")
    slot_grad = jnp.sum(parts.astype(F32), axis=0)
    rounded = slot_grad.astype(BF)
    partner = swap(rounded, "expert", slots // 2)
    grad_down = (slot_grad + partner.astype(F32))[None]

    half = jnp.dot(scaled, weight, preferred_element_type=F32)
    low, high = half[:rows], half[rows:]
    mine = jnp.where(first, low, high)
    theirs = jnp.where(first, high, low)
    theirs = swap(theirs, "core", 1)
    hidden, theirs = lax.optimization_barrier((hidden, theirs))
    gate, up, sig, silu, activation = swiglu(hidden)
    grad_act = mine + theirs
    grad_gate = grad_act * up * sig * (1.0 + gate * (1.0 - sig))
    grad_up = grad_act * silu
    grad_hidden = jnp.concatenate([grad_gate, grad_up], axis=1).astype(BF)[None]
    weighted = jnp.sum(grad_act * activation.astype(F32), axis=1)
    back = exchange(weighted.reshape(slots, cap), "expert").reshape(rows)
    grad_probs = (
        jnp.sum(jnp.where(place, back[None, :], 0.0), axis=1, keepdims=True) / probs
    )
    return (grad_down, grad_hidden, grad_probs)


def solution(mesh):
    slots, groups = mesh.shape["expert"], mesh.shape["dp"]
    fine = Mesh(mesh.devices.reshape(slots, groups // 2, 2), ("expert", "x", "core"))
    dp = ("x", "core")
    tok = P(("expert", "x", "core"), None)
    slot = P("expert", dp, None)

    return jax.shard_map(
        on_device,
        mesh=fine,
        in_specs=(tok, tok, tok, slot, slot),
        out_specs=(slot, slot, tok),
        check_vma=False,
    )
```

```python
import jax
import jax.numpy as jnp
import numpy as np
from jax import lax
from jax.sharding import Mesh, PartitionSpec as P


BF = jnp.bfloat16
F32 = jnp.float32
SPREAD = ("core", "expert")


def swap(block, axis, bit):
    count = lax.axis_size(axis)
    return lax.ppermute(block, axis, [(k, k ^ bit) for k in range(count)])


def fan(block, step):
    chips = lax.axis_size("x")
    route = [
        (chip * 2 + core, (chip + step - 2 * step * core) % chips * 2 + core)
        for chip in range(chips)
        for core in range(2)
    ]
    return lax.ppermute(block, ("x", "core"), route)


def exchange(blocks, axis):
    return lax.all_to_all(blocks, axis, split_axis=0, concat_axis=0, tiled=True)


def swiglu(hidden):
    ff = hidden.shape[1] // 2
    gate = hidden[:, :ff].astype(F32)
    up = hidden[:, ff:].astype(F32)
    sig = jax.nn.sigmoid(gate)
    silu = gate * sig
    return gate, up, sig, silu, (silu * up).astype(BF)


def on_device(cotangent, router_probs, slot_ids, saved_hidden, down_weight):
    slots = lax.axis_size("expert")
    chips = lax.axis_size("x")
    core = lax.axis_index("core")
    tokens, width = cotangent.shape
    cap = saved_hidden.shape[1] // slots
    lanes = width // (2 * chips)
    rows = slots * cap
    first = core == 0
    hidden = saved_hidden[0]
    ff = hidden.shape[1] // 2

    ids = slot_ids.reshape(-1)
    same = (ids[:, None] == ids[None, :]) & (
        jnp.arange(tokens)[None, :] < jnp.arange(tokens)[:, None]
    )
    position = jnp.sum(same.astype(jnp.int32), axis=1)
    row = np.arange(rows, dtype=np.int32)
    place = (ids[:, None] == (row // cap)[None, :]) & (
        position[:, None] == (row % cap)[None, :]
    )
    probs = router_probs.astype(F32)
    spread = jnp.where(place, probs, 0.0).astype(BF)
    sent = lax.dot_general(
        spread, cotangent, (((0,), (0,)), ((), ())), preferred_element_type=F32
    ).astype(BF)
    sent = sent.reshape(slots, cap, chips, 2, lanes).transpose(3, 0, 1, 2, 4)
    sent = sent.reshape(2 * slots, cap * chips, lanes)
    got = exchange(sent, SPREAD)
    scaled = got.reshape(2 * rows, chips * lanes)

    chip = lax.axis_index("x")
    ahead = jnp.where(first, -1, 1)
    mate = swap(down_weight[0], "core", 1)
    pair = jnp.concatenate([down_weight, mate[None]], axis=0)
    pieces = {0: down_weight[0]}
    relayed = []
    for step in range(1, chips // 2):
        got_pair = fan(pair, step)
        pieces[step] = got_pair[0]
        relayed.append(got_pair[1])
    far = fan(down_weight[0], chips // 2)
    pieces[chips // 2] = far
    relayed = swap(jnp.stack(relayed), "core", 1)
    for step in range(1, chips // 2):
        pieces[-step] = relayed[step - 1]
    weight = jnp.zeros((chips,) + down_weight.shape[1:], BF)
    for step, piece in pieces.items():
        weight = lax.dynamic_update_index_in_dim(
            weight, piece, jnp.bitwise_and(chip + ahead * step, chips - 1), 0
        )
    weight = weight.reshape(chips * lanes, ff)

    activation = swiglu(hidden)[-1]
    other_activation = swap(activation, "core", 1)
    both = jnp.concatenate(
        [
            jnp.where(first, activation, other_activation),
            jnp.where(first, other_activation, activation),
        ],
        axis=0,
    )

    partial = lax.dot_general(
        scaled, both, (((0,), (0,)), ((), ())), preferred_element_type=F32
    ).astype(BF)
    parts = exchange(partial.reshape(chips, lanes, ff), "x")
    slot_grad = jnp.sum(parts.astype(F32), axis=0)
    rounded = slot_grad.astype(BF)
    partner = swap(rounded, "expert", slots // 2)
    grad_down = (slot_grad + partner.astype(F32))[None]

    half = jnp.dot(scaled, weight, preferred_element_type=F32)
    low, high = half[:rows], half[rows:]
    mine = jnp.where(first, low, high)
    theirs = jnp.where(first, high, low)
    theirs = swap(theirs, "core", 1)
    hidden, theirs = lax.optimization_barrier((hidden, theirs))
    gate, up, sig, silu, activation = swiglu(hidden)
    grad_act = mine + theirs
    grad_gate = grad_act * up * sig * (1.0 + gate * (1.0 - sig))
    grad_up = grad_act * silu
    grad_hidden = jnp.concatenate([grad_gate, grad_up], axis=1).astype(BF)[None]
    weighted = jnp.sum(grad_act * activation.astype(F32), axis=1)
    sending = jnp.pad(weighted.reshape(slots, 1, cap), ((0, 0), (0, 0), (0, lanes - cap)))
    back = exchange(sending, "expert").reshape(slots, lanes)
    named = (ids[:, None] == jnp.arange(slots, dtype=jnp.int32)[None, :]).astype(F32)
    picked = jnp.dot(named, back, precision=lax.Precision.HIGHEST)
    lane = position[:, None] == jnp.arange(lanes, dtype=jnp.int32)[None, :]
    grad_probs = jnp.sum(jnp.where(lane, picked, 0.0), axis=1, keepdims=True) / probs
    return (grad_down, grad_hidden, grad_probs)


def solution(mesh):
    slots, groups = mesh.shape["expert"], mesh.shape["dp"]
    fine = Mesh(mesh.devices.reshape(slots, groups // 2, 2), ("expert", "x", "core"))
    dp = ("x", "core")
    tok = P(("expert", "x", "core"), None)
    slot = P("expert", dp, None)

    return jax.shard_map(
        on_device,
        mesh=fine,
        in_specs=(tok, tok, tok, slot, slot),
        out_specs=(slot, slot, tok),
        check_vma=False,
    )
```

```python
import jax
import jax.numpy as jnp
import numpy as np
from jax import lax
from jax.sharding import Mesh, PartitionSpec as P


BF = jnp.bfloat16
F32 = jnp.float32
SPREAD = ("core", "expert")


def swap(block, axis, bit):
    count = lax.axis_size(axis)
    return lax.ppermute(block, axis, [(k, k ^ bit) for k in range(count)])


def fan(block, step):
    chips = lax.axis_size("x")
    route = [
        (chip * 2 + core, (chip + step - 2 * step * core) % chips * 2 + core)
        for chip in range(chips)
        for core in range(2)
    ]
    return lax.ppermute(block, ("x", "core"), route)


def exchange(blocks, axis):
    return lax.all_to_all(blocks, axis, split_axis=0, concat_axis=0, tiled=True)


def swiglu(hidden):
    ff = hidden.shape[1] // 2
    gate = hidden[:, :ff].astype(F32)
    up = hidden[:, ff:].astype(F32)
    sig = jax.nn.sigmoid(gate)
    silu = gate * sig
    return gate, up, sig, silu, (silu * up).astype(BF)


def on_device(cotangent, router_probs, slot_ids, saved_hidden, down_weight):
    slots = lax.axis_size("expert")
    chips = lax.axis_size("x")
    core = lax.axis_index("core")
    tokens, width = cotangent.shape
    cap = saved_hidden.shape[1] // slots
    lanes = width // (2 * chips)
    rows = slots * cap
    first = core == 0
    hidden = saved_hidden[0]
    ff = hidden.shape[1] // 2

    ids = slot_ids.reshape(-1)
    same = (ids[:, None] == ids[None, :]) & (
        jnp.arange(tokens)[None, :] < jnp.arange(tokens)[:, None]
    )
    position = jnp.sum(same.astype(jnp.int32), axis=1)
    row = np.arange(rows, dtype=np.int32)
    place = (ids[:, None] == (row // cap)[None, :]) & (
        position[:, None] == (row % cap)[None, :]
    )
    probs = router_probs.astype(F32)
    spread = jnp.where(place, probs, 0.0).astype(BF)
    sent = lax.dot_general(
        spread, cotangent, (((0,), (0,)), ((), ())), preferred_element_type=F32
    ).astype(BF)
    sent = sent.reshape(slots, cap, chips, 2, lanes).transpose(3, 0, 1, 2, 4)
    sent = sent.reshape(2 * slots, cap * chips, lanes)
    got = exchange(sent, SPREAD)
    scaled = got.reshape(2 * rows, chips * lanes)

    chip = lax.axis_index("x")
    ahead = jnp.where(first, -1, 1)
    mate = swap(down_weight[0], "core", 1)
    pair = jnp.concatenate([down_weight, mate[None]], axis=0)
    pieces = {0: down_weight[0]}
    relayed = []
    for step in range(1, chips // 2):
        got_pair = fan(pair, step)
        pieces[step] = got_pair[0]
        relayed.append(got_pair[1])
    far = fan(down_weight[0], chips // 2)
    pieces[chips // 2] = far
    relayed = swap(jnp.stack(relayed), "core", 1)
    for step in range(1, chips // 2):
        pieces[-step] = relayed[step - 1]
    weight = jnp.zeros((chips,) + down_weight.shape[1:], BF)
    for step, piece in pieces.items():
        weight = lax.dynamic_update_index_in_dim(
            weight, piece, jnp.bitwise_and(chip + ahead * step, chips - 1), 0
        )
    weight = weight.reshape(chips * lanes, ff)

    activation = swiglu(hidden)[-1]
    other_activation = swap(activation, "core", 1)
    both = jnp.concatenate(
        [
            jnp.where(first, activation, other_activation),
            jnp.where(first, other_activation, activation),
        ],
        axis=0,
    )

    partial = lax.dot_general(
        scaled, both, (((0,), (0,)), ((), ())), preferred_element_type=F32
    ).astype(BF)
    parts = exchange(partial.reshape(chips, lanes, ff), "x")
    slot_grad = jnp.sum(parts.astype(F32), axis=0)
    rounded = slot_grad.astype(BF)
    partner = swap(rounded, "expert", slots // 2)
    grad_down = (slot_grad + partner.astype(F32))[None]

    half = jnp.dot(scaled, weight, preferred_element_type=F32)
    low, high = half[:rows], half[rows:]
    mine = jnp.where(first, low, high)
    theirs = jnp.where(first, high, low)
    theirs = swap(theirs, "core", 1)
    hidden, theirs = lax.optimization_barrier((hidden, theirs))
    gate, up, sig, silu, activation = swiglu(hidden)
    grad_act = mine + theirs
    grad_gate = grad_act * up * sig * (1.0 + gate * (1.0 - sig))
    grad_up = grad_act * silu
    grad_hidden = jnp.concatenate([grad_gate, grad_up], axis=1).astype(BF)[None]
    weighted = jnp.sum(grad_act * activation.astype(F32), axis=1)
    sending = jnp.pad(weighted.reshape(slots, 1, cap), ((0, 0), (0, 0), (0, lanes - cap)))
    back = exchange(sending, "expert").reshape(slots, lanes)
    slot_row = jnp.arange(slots, dtype=jnp.int32)[None, :]
    named = jnp.where(ids[:, None] == slot_row, 1.0 / probs, 0.0)
    picked = jnp.dot(named, back, precision=lax.Precision.HIGHEST)
    lane = position[:, None] == jnp.arange(lanes, dtype=jnp.int32)[None, :]
    grad_probs = jnp.sum(jnp.where(lane, picked, 0.0), axis=1, keepdims=True)
    return (grad_down, grad_hidden, grad_probs)


def solution(mesh):
    slots, groups = mesh.shape["expert"], mesh.shape["dp"]
    fine = Mesh(mesh.devices.reshape(slots, groups // 2, 2), ("expert", "x", "core"))
    dp = ("x", "core")
    tok = P(("expert", "x", "core"), None)
    slot = P("expert", dp, None)

    return jax.shard_map(
        on_device,
        mesh=fine,
        in_specs=(tok, tok, tok, slot, slot),
        out_specs=(slot, slot, tok),
        check_vma=False,
    )
```
